32 devices in a mesh: expert: 8 (over y, x, core), replica: 4 (over z).
Axes of the slice: x: 2, y: 2, z: 4, core: 2. Of those that a mesh axis runs over, the one named last changes fastest.
Arguments:
- tokens: bfloat16 [8192, 7168], P(('expert', 'replica')), may hold values from -40 to 40
- routes: int32 [8192, 8], P(('expert', 'replica')), may hold values from 0 to 255, all different within a row
- gate_weight: bfloat16 [7168, 4096], P(None, 'expert'), may hold values from -0.0625 to 0.0625
- up_weight: bfloat16 [7168, 4096], P(None, 'expert'), may hold values from -0.0625 to 0.0625
Outputs:
- calibrated: bfloat16 [512, 4096], P(('expert', 'replica'))
The draws below stay inside these ranges and needn't reach their ends.
Inputs may be any that keep to these rules, and one draw needn't show every extreme that they name: `routes`: each row names 8 different experts of the layer, and every expert is named by some row.
All inputs are finite; a program needn't handle non-finite values.
Results may differ from the reference program's by a relative error of at most 0.001.
Values may be sent and summed in bfloat16 or wider, within the bound.
A program may use at most 128 MiB of HBM per device.

```python
import math
import jax
import jax.numpy as jnp
from jax import lax

D = 7168
FF = 2048
ROUTED = 256
TOP = 8
CAP = 16
KMOM = 12
QITERS = 4
TOK_DEV = 256
EXPERTS = 2
TOKENS = 8192
N_EXPERT = 8
N_REPLICA = 4


def draw_tokens(key, part):
    key_base = jax.random.fold_in(key, 0)
    key_scale = jax.random.fold_in(key, 2)
    source = jnp.arange(TOKENS, dtype=jnp.int32) // TOK_DEV
    replica_pos = (source % N_REPLICA).astype(jnp.float32)
    replica_ramp = jnp.sqrt(1.0 + 2.0 * replica_pos / max(N_REPLICA - 1, 1))
    values = jax.random.truncated_normal(key_base, -6.0, 6.0, (TOKENS, D), jnp.float32)
    spread = jnp.exp(jax.random.uniform(key_scale, (TOKENS,), jnp.float32, -0.5, 0.5) * math.log(10.0))
    return (values * (spread * replica_ramp)[:, None]).astype(jnp.bfloat16)


def block_scale(stream_key, extent, pieces, low, high):
    loudness, own = 1.0, jax.random.fold_in(stream_key, 6)
    for dim, shards_of in pieces:
        draws = jnp.exp(jax.random.uniform(jax.random.fold_in(own, dim), (shards_of,), jnp.float32, low / len(pieces), high / len(pieces)))
        loudness = loudness * jnp.repeat(draws, extent[dim] // shards_of).reshape([-1 if axis == dim else 1 for axis in range(len(extent))])
    return loudness


def choose_distinct(stream_key, rows, amount, top, lift):
    ranking = jax.random.permutation(jax.random.fold_in(stream_key, 1), amount)
    pull = ranking
    for power in range(3):
        pull = pull * pull // amount
    pull = pull * lift // amount
    chance = jax.random.randint(jax.random.fold_in(stream_key, 2), (rows, amount), 0, 4096) + pull
    sure = jax.random.permutation(jax.random.fold_in(stream_key, 3), rows)[jnp.arange(amount) % rows]
    chance = jnp.where(jnp.arange(rows)[:, None] == sure[None, :], 1 << 14, chance)
    priority = chance * amount + jnp.arange(amount)
    return lax.top_k(priority.astype(jnp.int32), top)[1].astype(jnp.int32)


def noise(key, dims, deviation, limit, cuts=(), held_as=jnp.bfloat16):
    values = deviation * jax.random.normal(key, dims, jnp.float32)
    if cuts:
        values = values * block_scale(key, dims, cuts, -0.22, 0.18)
    return jnp.clip(values, -limit, limit).astype(held_as)


def setup_inputs(seed: int = 0) -> dict:
    splits = jax.random.split(jax.random.key(seed), 5)
    return {
        "tokens": draw_tokens(jax.random.fold_in(splits[4], 71), 0),
        "routes": choose_distinct(splits[1], TOKENS, ROUTED, TOP, 256),
        "gate_weight": noise(splits[2], (D, EXPERTS * FF), D ** -0.5, 0.0625, ((1, 8),)),
        "up_weight": noise(splits[3], (D, EXPERTS * FF), D ** -0.5, 0.0625, ((1, 8),)),
    }


QUANTILE_LEVEL = 0.99
EPSILON = 1e-6


def slot_table(route_block):
    window = jnp.arange(EXPERTS, dtype=jnp.int32)
    naming = jnp.sum((route_block[:, :, None] == window[None, None, :]).astype(jnp.int32), axis=1)
    before = jnp.cumsum(naming, axis=0) - naming
    positions = jnp.arange(CAP, dtype=jnp.int32)
    chosen = naming[:, :, None] * (before[:, :, None] == positions[None, None, :]).astype(jnp.int32)
    token_ids = jnp.arange(route_block.shape[0], dtype=jnp.int32)
    picked = jnp.sum(chosen * token_ids[:, None, None], axis=0)
    filled = jnp.sum(chosen, axis=0)
    return picked, filled


def chebyshev_sums(scaled, occupied):
    previous = jnp.ones_like(scaled)
    current = scaled
    totals = [jnp.sum(occupied[:, None] * previous, axis=0), jnp.sum(occupied[:, None] * current, axis=0)]
    for degree in range(2, KMOM):
        previous, current = current, 2.0 * scaled * current - previous
        totals.append(jnp.sum(occupied[:, None] * current, axis=0))
    return jnp.stack(totals[:KMOM])


def clip_fraction(moments, counted):
    coefficient = moments[1:] / counted[None, :]
    orders = jnp.arange(1, KMOM, dtype=jnp.float32)[:, None]
    angles = jnp.full(moments.shape[1:], 0.5 * math.pi, jnp.float32)
    for iteration in range(QITERS):
        lower_mass = 1.0 - angles / math.pi - (2.0 / math.pi) * jnp.sum(coefficient * jnp.sin(orders * angles[None, :]) / orders, axis=0)
        angles = angles + math.pi * (lower_mass - QUANTILE_LEVEL)
    return 0.5 * (1.0 + jnp.cos(angles))


def take_block(packed):
    tok_block, slot_ids, occupied = packed
    gathered = jnp.take(tok_block, slot_ids.reshape(-1), axis=0).reshape(EXPERTS, CAP, D)
    return jnp.where(occupied[:, :, None] > 0, gathered, jnp.zeros_like(gathered))


def reference(tokens, routes, gate_weight, up_weight):
    sources = N_EXPERT * N_REPLICA
    tok_blocks = tokens.reshape(sources, TOK_DEV, D)
    route_blocks = routes.reshape(sources, TOK_DEV, TOP)
    picked, filled = lax.map(slot_table, route_blocks)
    dispatched = lax.map(take_block, (tok_blocks, picked, filled))

    def one_expert(expert_id):
        slab = lax.dynamic_index_in_dim(dispatched, expert_id, 1, keepdims=False).reshape(sources * CAP, D)
        occupied = lax.dynamic_index_in_dim(filled, expert_id, 1, keepdims=False).reshape(sources * CAP).astype(jnp.float32)
        gate_cols = lax.dynamic_slice_in_dim(gate_weight, expert_id * FF, FF, 1)
        up_cols = lax.dynamic_slice_in_dim(up_weight, expert_id * FF, FF, 1)
        gate_act = jnp.dot(slab, gate_cols, preferred_element_type=jnp.float32)
        up_act = jnp.dot(slab, up_cols, preferred_element_type=jnp.float32)
        hidden = jax.nn.silu(gate_act) * up_act
        magnitude = jnp.abs(hidden)
        ceiling = jnp.max(magnitude, axis=0) + EPSILON
        scaled = 2.0 * magnitude / ceiling - 1.0
        moments = chebyshev_sums(scaled, occupied)
        clip_level = ceiling * clip_fraction(moments, moments[0])
        result = jnp.clip(hidden, -clip_level, clip_level) / ceiling
        return result.astype(jnp.bfloat16).reshape(sources, CAP, FF)

    results = lax.map(one_expert, jnp.arange(EXPERTS, dtype=jnp.int32))
    return results.transpose(1, 2, 0, 3).reshape(sources * CAP, EXPERTS * FF)
```

```python
import functools
import math

import jax
import jax.numpy as jnp
from jax import lax
from jax.experimental import pallas as pl
from jax.experimental.pallas import tpu as pltpu
from jax.sharding import PartitionSpec as P

HSPLIT = 4
CAP = 16
KMOM = 12
QITERS = 4
LANES = 128
CHUNK = 1024
ROWS = 32

QUANTILE_LEVEL = 0.99
EPSILON = 1e-06
MESH = pl.DeviceIdType.MESH

PI_HIGH = 3.140625
PI_LOW = math.pi - PI_HIGH
SIN_TERMS = [(-1.0) ** i / math.factorial(2 * i + 1) for i in range(7)]
COS_TERMS = [(-1.0) ** i / math.factorial(2 * i) for i in range(8)]


def horner(square, terms):
    total = jnp.full_like(square, terms[-1])
    for term in terms[-2::-1]:
        total = total * square + term
    return total


def sin_cos(angle):
    turns = jnp.floor(angle * (1.0 / math.pi) + 0.5)
    rest = (angle - turns * PI_HIGH) - turns * PI_LOW
    sign = 1.0 - 2.0 * (turns - 2.0 * jnp.floor(turns * 0.5))
    square = rest * rest
    return sign * rest * horner(square, SIN_TERMS), sign * horner(square, COS_TERMS)


def clip_fraction(coefficient):
    start = (1.0 - QUANTILE_LEVEL) * math.pi
    total = jnp.zeros_like(coefficient[0])
    for k in range(1, KMOM, 2):
        total = total + coefficient[k - 1] * ((1.0 if k % 4 == 1 else -1.0) / k)
    angle = start - 2.0 * total
    for _ in range(QITERS - 1):
        sine, cosine = sin_cos(angle)
        double = 2.0 * cosine
        before, current = jnp.zeros_like(sine), sine
        total = jnp.zeros_like(sine)
        for k in range(1, KMOM):
            total = total + coefficient[k - 1] * (current * (1.0 / k))
            before, current = current, double * current - before
        angle = start - 2.0 * total
    return 0.5 * (1.0 + sin_cos(angle)[1])


def rebase(moments, ratio):
    shift = ratio - 1.0
    before = moments
    current = [
        0.5 * ratio * (before[j + 1] + before[abs(j - 1)]) + shift * before[j]
        for j in range(KMOM - 1)
    ]
    out = [current[0]]
    twice = 2.0 * shift
    for k in range(1, KMOM - 1):
        following = [
            ratio * (current[j + 1] + current[abs(j - 1)]) + twice * current[j] - before[j]
            for j in range(KMOM - 1 - k)
        ]
        before, current = current, following
        out.append(current[0])
    return out


def kernel(
    devices, replicas, chunks,
    tok, rt, wg, wu, out,
    T, RT, SEL, Y, OY, X, OX, WG, WU, AG, AU, H, SK, CNT, RES,
    tok_sem, rt_sem, wg_sem, wu_sem,
    x_send, x_recv, o_send, o_recv, f_send, f_recv, fo_sem,
    s_send, s_recv, n_send, n_recv, r_send, r_recv, own_sem,
):
    groups = devices // HSPLIT
    half = devices // 2 * CAP
    width = WG.shape[1]
    tiles = width // LANES
    rows = devices * CAP
    me = lax.axis_index("expert")
    z = lax.axis_index("replica")
    c = me % 2
    p = (me // 2) % 2
    a = me // HSPLIT
    partner = me + 1 - 2 * c

    def pos(j):
        return (j % 2) * (devices // 2) + j // 2

    def other(dg, dp, dc):
        return HSPLIT * ((a + dg) % groups) + 2 * ((p + dp) % 2) + (c + dc) % 2

    combos = [(dg, dp) for dg in range(groups) for dp in range(2) if (dg, dp) != (0, 0)]
    combos = combos[::-1]
    alls = [
        (dg, dp, dc)
        for dg in range(groups) for dp in range(2) for dc in range(2)
        if (dg, dp, dc) != (0, 0, 0)
    ]

    def block(j):
        return pl.ds(pl.multiple_of(pos(j) * CAP, CAP), CAP)

    def load_tokens(ch):
        return pltpu.make_async_copy(
            tok.at[:, pl.ds(pl.multiple_of(ch * CHUNK, CHUNK), CHUNK)], T.at[ch], tok_sem.at[ch])

    def load_weights(ch):
        part = pl.ds(pl.multiple_of(ch * CHUNK, CHUNK), CHUNK)
        return (
            pltpu.make_async_copy(wg.at[part], WG.at[part], wg_sem.at[ch]),
            pltpu.make_async_copy(wu.at[part], WU.at[part], wu_sem.at[ch]),
        )

    load_routes = pltpu.make_async_copy(rt, RT, rt_sem)
    load_routes.start()
    for ch in range(chunks):
        load_tokens(ch).start()

    barrier = pltpu.get_barrier_semaphore()
    for combo in alls:
        pl.semaphore_signal(barrier, inc=1, device_id=(other(*combo), z), device_id_type=MESH)
    for dz in range(1, replicas):
        pl.semaphore_signal(
            barrier, inc=1, device_id=(me, (z + dz) % replicas), device_id_type=MESH)

    for ch in range(chunks):
        for copy in load_weights(ch):
            copy.start()

    load_routes.wait()
    routes = RT[...]
    count = routes.shape[1]
    t_from = lax.broadcasted_iota(jnp.int32, (count, count), 0)
    t_to = lax.broadcasted_iota(jnp.int32, (count, count), 1)
    earlier = jnp.where(t_from < t_to, 1.0, 0.0).astype(jnp.bfloat16)
    named = [
        jnp.sum(jnp.where(routes == (a + dg) % groups, 1.0, 0.0), axis=0, keepdims=True)
        for dg in range(groups)
    ]
    table = jnp.concatenate(
        [jnp.broadcast_to(n, (CAP, count)) for n in named], axis=0)
    before = jnp.dot(table.astype(jnp.bfloat16), earlier, preferred_element_type=jnp.float32)
    slot = (lax.broadcasted_iota(jnp.int32, (groups * CAP, count), 0) % CAP).astype(jnp.float32)
    picks = jnp.where(before == slot, table, 0.0)
    SEL[...] = picks.astype(jnp.bfloat16)
    filled = jnp.broadcast_to(
        jnp.sum(picks, axis=1, keepdims=True), (groups * CAP, LANES)).astype(jnp.bfloat16)
    OY[...] = filled
    OX[block(me), :] = filled[:CAP]

    def gather(ch):
        load_tokens(ch).wait()
        picked = jnp.dot(
            SEL[...], T[ch], preferred_element_type=jnp.float32).astype(jnp.bfloat16)
        Y[ch] = picked
        X[ch, block(me), :] = picked[:CAP]

    def send_rows(ch, i):
        dg, dp = combos[i]
        return pltpu.make_async_remote_copy(
            src_ref=Y.at[ch, pl.ds(dg * CAP, CAP), :], dst_ref=X.at[ch, block(me), :],
            send_sem=x_send.at[ch, i], recv_sem=x_recv.at[ch, i],
            device_id=(other(dg, dp, 0), z), device_id_type=MESH)

    def send_filled(i):
        dg, dp = combos[i]
        return pltpu.make_async_remote_copy(
            src_ref=OY.at[pl.ds(dg * CAP, CAP), :], dst_ref=OX.at[block(me), :],
            send_sem=o_send.at[i], recv_sem=o_recv.at[i],
            device_id=(other(dg, dp, 0), z), device_id_type=MESH)

    def forward_rows(ch):
        part = pl.ds(pl.multiple_of(c * half, half), half)
        return pltpu.make_async_remote_copy(
            src_ref=X.at[ch, part, :], dst_ref=X.at[ch, part, :],
            send_sem=f_send.at[ch], recv_sem=f_recv.at[ch],
            device_id=(partner, z), device_id_type=MESH)

    def forward_filled():
        part = pl.ds(pl.multiple_of(c * half, half), half)
        return pltpu.make_async_remote_copy(
            src_ref=OX.at[part, :], dst_ref=OX.at[part, :],
            send_sem=fo_sem.at[0], recv_sem=fo_sem.at[1],
            device_id=(partner, z), device_id_type=MESH)

    gather(0)
    pl.semaphore_wait(barrier, len(alls) + replicas - 1)
    for i in range(len(combos)):
        send_filled(i).start()

    def sending(ch, _):
        gather(ch + 1)
        for i in range(len(combos)):
            send_rows(ch, i).start()
        return 0

    lax.fori_loop(0, chunks - 1, sending, 0)
    for i in range(len(combos)):
        send_rows(chunks - 1, i).start()

    for i in range(len(combos)):
        send_filled(i).wait_recv()
    forward_filled().start()

    def collect(ch):
        for i in range(len(combos)):
            send_rows(ch, i).wait_recv()
        forward_rows(ch).start()

    def multiply(ch, first):
        forward_rows(ch).wait_recv()
        for copy in load_weights(ch):
            copy.wait()
        part = pl.ds(pl.multiple_of(ch * CHUNK, CHUNK), CHUNK)
        x = X[ch]
        for W, A in ((WG, AG), (WU, AU)):
            product = jnp.dot(x, W[part, :], preferred_element_type=jnp.float32)
            A[...] = product if first else A[...] + product

    collect(0)
    collect(1)
    multiply(0, True)

    forward_filled().wait()
    total = jnp.sum(OX[...].astype(jnp.float32), axis=0, keepdims=True)
    CNT[z] = jnp.broadcast_to(total, (8, LANES))

    def step(ch, _):
        collect(ch + 1)
        multiply(ch, False)
        return 0

    lax.fori_loop(1, chunks - 1, step, 0)

    def send_count(dz):
        return pltpu.make_async_remote_copy(
            src_ref=CNT.at[z], dst_ref=CNT.at[z],
            send_sem=n_send.at[dz - 1], recv_sem=n_recv.at[dz - 1],
            device_id=(me, (z + dz) % replicas), device_id_type=MESH)

    for dz in range(1, replicas):
        send_count(dz).start()
    multiply(chunks - 1, False)

    def activate(i, top):
        part = pl.ds(pl.multiple_of(i * ROWS, ROWS), ROWS)
        g = AG[part, :]
        h = g / (1.0 + jnp.exp(-g)) * AU[part, :]
        H[part, :] = h
        return jnp.maximum(top, jnp.max(jnp.abs(h).reshape(ROWS // 8, 8, width), axis=0))

    top = lax.fori_loop(0, rows // ROWS, activate, jnp.zeros((8, width), jnp.float32))
    ceiling = jnp.max(top, axis=0, keepdims=True) + EPSILON
    scale = 2.0 / ceiling
    for l in range(tiles):
        lanes = slice(l * LANES, (l + 1) * LANES)
        scale_l = scale[:, lanes]

        def sketch(i, sums):
            part = pl.ds(pl.multiple_of(i * ROWS, ROWS), ROWS)
            scaled = jnp.abs(H[part, lanes]) * scale_l - 1.0
            double = 2.0 * scaled
            previous = OX[part, :].astype(jnp.float32)
            current = previous * scaled
            new = []
            for k in range(KMOM - 1):
                new.append(sums[k] + jnp.sum(current.reshape(ROWS // 8, 8, LANES), axis=0))
                previous, current = current, double * current - previous
            return tuple(new)

        zero = jnp.zeros((8, LANES), jnp.float32)
        sums = lax.fori_loop(0, rows // ROWS, sketch, (zero,) * (KMOM - 1))
        SK[z, l:l + 1, :] = ceiling[:, lanes]
        for k in range(1, KMOM):
            SK[z, k * tiles + l:k * tiles + l + 1, :] = jnp.sum(
                sums[k - 1], axis=0, keepdims=True)

    def send_sketch(dz):
        return pltpu.make_async_remote_copy(
            src_ref=SK.at[z], dst_ref=SK.at[z],
            send_sem=s_send.at[dz - 1], recv_sem=s_recv.at[dz - 1],
            device_id=(me, (z + dz) % replicas), device_id_type=MESH)

    for dz in range(1, replicas):
        send_sketch(dz).start()
    for dz in range(1, replicas):
        send_count(dz).wait()
    for dz in range(1, replicas):
        send_sketch(dz).wait()

    def across(k):
        return [SK[r, k * tiles:(k + 1) * tiles, :] for r in range(replicas)]

    local = across(0)
    common = functools.reduce(jnp.maximum, local)
    ratio = jnp.concatenate([value / common for value in local], axis=0)
    moments = [jnp.concatenate([CNT[r, :tiles, :] for r in range(replicas)], axis=0)]
    moments += [jnp.concatenate(across(k), axis=0) for k in range(1, KMOM)]

    def added(value):
        return functools.reduce(
            jnp.add, [value[r * tiles:(r + 1) * tiles] for r in range(replicas)])

    weight = 1.0 / added(moments[0])
    level = clip_fraction([added(value) * weight for value in rebase(moments, ratio)])
    level = common * level
    inverse = 1.0 / common

    for l in range(tiles):
        lanes = slice(l * LANES, (l + 1) * LANES)
        bound = level[l:l + 1]
        factor = inverse[l:l + 1]

        def finish(i, _):
            part = pl.ds(pl.multiple_of(i * ROWS, ROWS), ROWS)
            h = jnp.minimum(jnp.maximum(H[part, lanes], -bound), bound)
            RES[part, lanes] = (h * factor).astype(jnp.bfloat16)
            return 0

        lax.fori_loop(0, rows // ROWS, finish, 0)

    mine = pl.ds(pl.multiple_of(me * width, width), width)

    def send_result(i):
        j = other(*alls[i])
        return pltpu.make_async_remote_copy(
            src_ref=RES.at[block(j), :], dst_ref=out.at[:, mine],
            send_sem=r_send.at[i], recv_sem=r_recv.at[i],
            device_id=(j, z), device_id_type=MESH)

    for i in range(len(alls))[::-1]:
        send_result(i).start()
    keep = pltpu.make_async_copy(RES.at[block(me), :], out.at[:, mine], own_sem)
    keep.start()

    def drain(ch, _):
        for i in range(len(combos)):
            send_rows(ch, i).wait_send()
        forward_rows(ch).wait_send()
        return 0

    lax.fori_loop(0, chunks, drain, 0)
    for i in range(len(combos)):
        send_filled(i).wait_send()
    keep.wait()
    for i in range(len(alls)):
        send_result(i).wait()


def shards(tokens, routes, gate_weight, up_weight):
    devices = lax.axis_size("expert")
    replicas = lax.axis_size("replica")
    groups = devices // HSPLIT
    count, depth = tokens.shape
    width = gate_weight.shape[1]
    chunks = depth // CHUNK
    rows = devices * CAP
    near = devices // 2 - 1
    tiles = width // LANES
    bf16, f32 = jnp.bfloat16, jnp.float32
    dma = pltpu.SemaphoreType.DMA
    anywhere = pl.BlockSpec(memory_space=pl.ANY)
    return pl.pallas_call(
        functools.partial(kernel, devices, replicas, chunks),
        out_shape=jax.ShapeDtypeStruct((CAP, devices * width), bf16),
        in_specs=[anywhere] * 4,
        out_specs=anywhere,
        scratch_shapes=[
            pltpu.VMEM((chunks, count, CHUNK), bf16),
            pltpu.VMEM((routes.shape[1], count), jnp.int32),
            pltpu.VMEM((groups * CAP, count), bf16),
            pltpu.VMEM((chunks, groups * CAP, CHUNK), bf16),
            pltpu.VMEM((groups * CAP, LANES), bf16),
            pltpu.VMEM((chunks, rows, CHUNK), bf16),
            pltpu.VMEM((rows, LANES), bf16),
            pltpu.VMEM((depth, width), bf16),
            pltpu.VMEM((depth, width), bf16),
            pltpu.VMEM((rows, width), f32),
            pltpu.VMEM((rows, width), f32),
            pltpu.VMEM((rows, width), f32),
            pltpu.VMEM((replicas, KMOM * tiles, LANES), f32),
            pltpu.VMEM((replicas, 8, LANES), f32),
            pltpu.VMEM((rows, width), bf16),
            dma((chunks,)), dma(()), dma((chunks,)), dma((chunks,)),
            dma((chunks, near)), dma((chunks, near)), dma((near,)), dma((near,)),
            dma((chunks,)), dma((chunks,)), dma((2,)),
            dma((replicas - 1,)), dma((replicas - 1,)),
            dma((replicas - 1,)), dma((replicas - 1,)),
            dma((devices - 1,)), dma((devices - 1,)), dma(()),
        ],
        compiler_params=pltpu.CompilerParams(
            collective_id=0, has_side_effects=True, vmem_limit_bytes=60 * 1024 * 1024),
    )(tokens, routes.T, gate_weight, up_weight)


def solution(mesh):
    in_specs = (
        P(("expert", "replica"), None),
        P(("expert", "replica"), None),
        P(None, "expert"),
        P(None, "expert"),
    )
    out_specs = P(("expert", "replica"), None)
    return jax.shard_map(shards, mesh=mesh, in_specs=in_specs, out_specs=out_specs, check_vma=False)
```

```python
import functools
import math

import jax
import jax.numpy as jnp
from jax import lax
from jax.experimental import pallas as pl
from jax.experimental.pallas import tpu as pltpu
from jax.sharding import PartitionSpec as P

HSPLIT = 4
CAP = 16
KMOM = 12
QITERS = 4
LANES = 128
CHUNK = 512
ROWS = 32

QUANTILE_LEVEL = 0.99
EPSILON = 1e-06
MESH = pl.DeviceIdType.MESH

PI_HIGH = 3.140625
PI_LOW = math.pi - PI_HIGH
SIN_TERMS = [(-1.0) ** i / math.factorial(2 * i + 1) for i in range(7)]
COS_TERMS = [(-1.0) ** i / math.factorial(2 * i) for i in range(8)]


def horner(square, terms):
    total = jnp.full_like(square, terms[-1])
    for term in terms[-2::-1]:
        total = total * square + term
    return total


def sin_cos(angle):
    turns = jnp.floor(angle * (1.0 / math.pi) + 0.5)
    rest = (angle - turns * PI_HIGH) - turns * PI_LOW
    sign = 1.0 - 2.0 * (turns - 2.0 * jnp.floor(turns * 0.5))
    square = rest * rest
    return sign * rest * horner(square, SIN_TERMS), sign * horner(square, COS_TERMS)


def clip_fraction(coefficient):
    start = (1.0 - QUANTILE_LEVEL) * math.pi
    total = jnp.zeros_like(coefficient[0])
    for k in range(1, KMOM, 2):
        total = total + coefficient[k - 1] * ((1.0 if k % 4 == 1 else -1.0) / k)
    angle = start - 2.0 * total
    for _ in range(QITERS - 1):
        sine, cosine = sin_cos(angle)
        double = 2.0 * cosine
        before, current = jnp.zeros_like(sine), sine
        total = jnp.zeros_like(sine)
        for k in range(1, KMOM):
            total = total + coefficient[k - 1] * (current * (1.0 / k))
            before, current = current, double * current - before
        angle = start - 2.0 * total
    return 0.5 * (1.0 + sin_cos(angle)[1])


def rebase(moments, ratio):
    shift = ratio - 1.0
    before = moments
    current = [
        0.5 * ratio * (before[j + 1] + before[abs(j - 1)]) + shift * before[j]
        for j in range(KMOM - 1)
    ]
    out = [current[0]]
    twice = 2.0 * shift
    for k in range(1, KMOM - 1):
        following = [
            ratio * (current[j + 1] + current[abs(j - 1)]) + twice * current[j] - before[j]
            for j in range(KMOM - 1 - k)
        ]
        before, current = current, following
        out.append(current[0])
    return out


def kernel(
    devices, replicas, chunks,
    tok, rt, wg, wu, HB, LV,
    T, RT, SEL, Y, OY, X, OX, WG, WU, AG, AU, H, SK, CNT, LS,
    tok_sem, rt_sem, wg_sem, wu_sem,
    x_send, x_recv, o_send, o_recv, f_send, f_recv, fo_sem,
    s_send, s_recv, n_send, n_recv, h_send, h_recv, l_send, l_recv, own_sem,
):
    groups = devices // HSPLIT
    half = devices // 2 * CAP
    width = WG.shape[1]
    tiles = width // LANES
    rows = devices * CAP
    me = lax.axis_index("expert")
    z = lax.axis_index("replica")
    c = me % 2
    p = (me // 2) % 2
    a = me // HSPLIT
    partner = me + 1 - 2 * c

    def pos(j):
        return (j % 2) * (devices // 2) + j // 2

    def other(dg, dp, dc):
        return HSPLIT * ((a + dg) % groups) + 2 * ((p + dp) % 2) + (c + dc) % 2

    combos = [(dg, dp) for dg in range(groups) for dp in range(2) if (dg, dp) != (0, 0)]
    combos = combos[::-1]
    alls = [
        (dg, dp, dc)
        for dg in range(groups) for dp in range(2) for dc in range(2)
        if (dg, dp, dc) != (0, 0, 0)
    ]

    def block(j):
        return pl.ds(pl.multiple_of(pos(j) * CAP, CAP), CAP)

    def load_tokens(ch):
        return pltpu.make_async_copy(
            tok.at[:, pl.ds(pl.multiple_of(ch * CHUNK, CHUNK), CHUNK)], T.at[ch], tok_sem.at[ch])

    def load_weights(ch):
        part = pl.ds(pl.multiple_of(ch * CHUNK, CHUNK), CHUNK)
        return (
            pltpu.make_async_copy(wg.at[part], WG.at[part], wg_sem.at[ch]),
            pltpu.make_async_copy(wu.at[part], WU.at[part], wu_sem.at[ch]),
        )

    load_routes = pltpu.make_async_copy(rt, RT, rt_sem)
    load_routes.start()
    for ch in range(chunks):
        load_tokens(ch).start()

    barrier = pltpu.get_barrier_semaphore()
    for combo in alls:
        pl.semaphore_signal(barrier, inc=1, device_id=(other(*combo), z), device_id_type=MESH)
    for dz in range(1, replicas):
        pl.semaphore_signal(
            barrier, inc=1, device_id=(me, (z + dz) % replicas), device_id_type=MESH)

    for ch in range(chunks):
        for copy in load_weights(ch):
            copy.start()

    load_routes.wait()
    routes = RT[...]
    count = routes.shape[1]
    t_from = lax.broadcasted_iota(jnp.int32, (count, count), 0)
    t_to = lax.broadcasted_iota(jnp.int32, (count, count), 1)
    earlier = jnp.where(t_from < t_to, 1.0, 0.0).astype(jnp.bfloat16)
    named = [
        jnp.sum(jnp.where(routes == (a + dg) % groups, 1.0, 0.0), axis=0, keepdims=True)
        for dg in range(groups)
    ]
    table = jnp.concatenate(
        [jnp.broadcast_to(n, (CAP, count)) for n in named], axis=0)
    before = jnp.dot(table.astype(jnp.bfloat16), earlier, preferred_element_type=jnp.float32)
    slot = (lax.broadcasted_iota(jnp.int32, (groups * CAP, count), 0) % CAP).astype(jnp.float32)
    picks = jnp.where(before == slot, table, 0.0)
    SEL[...] = picks.astype(jnp.bfloat16)
    filled = jnp.broadcast_to(
        jnp.sum(picks, axis=1, keepdims=True), (groups * CAP, LANES)).astype(jnp.bfloat16)
    OY[...] = filled
    OX[block(me), :] = filled[:CAP]

    def gather(ch):
        load_tokens(ch).wait()
        picked = jnp.dot(
            SEL[...], T[ch], preferred_element_type=jnp.float32).astype(jnp.bfloat16)
        Y[ch] = picked
        X[ch, block(me), :] = picked[:CAP]

    def send_rows(ch, i):
        dg, dp = combos[i]
        return pltpu.make_async_remote_copy(
            src_ref=Y.at[ch, pl.ds(dg * CAP, CAP), :], dst_ref=X.at[ch, block(me), :],
            send_sem=x_send.at[ch, i], recv_sem=x_recv.at[ch, i],
            device_id=(other(dg, dp, 0), z), device_id_type=MESH)

    def send_filled(i):
        dg, dp = combos[i]
        return pltpu.make_async_remote_copy(
            src_ref=OY.at[pl.ds(dg * CAP, CAP), :], dst_ref=OX.at[block(me), :],
            send_sem=o_send.at[i], recv_sem=o_recv.at[i],
            device_id=(other(dg, dp, 0), z), device_id_type=MESH)

    def forward_rows(ch):
        part = pl.ds(pl.multiple_of(c * half, half), half)
        return pltpu.make_async_remote_copy(
            src_ref=X.at[ch, part, :], dst_ref=X.at[ch, part, :],
            send_sem=f_send.at[ch], recv_sem=f_recv.at[ch],
            device_id=(partner, z), device_id_type=MESH)

    def forward_filled():
        part = pl.ds(pl.multiple_of(c * half, half), half)
        return pltpu.make_async_remote_copy(
            src_ref=OX.at[part, :], dst_ref=OX.at[part, :],
            send_sem=fo_sem.at[0], recv_sem=fo_sem.at[1],
            device_id=(partner, z), device_id_type=MESH)

    gather(0)
    pl.semaphore_wait(barrier, len(alls) + replicas - 1)
    for i in range(len(combos)):
        send_filled(i).start()

    def sending(ch, _):
        gather(ch + 1)
        for i in range(len(combos)):
            send_rows(ch, i).start()
        return 0

    lax.fori_loop(0, chunks - 1, sending, 0)
    for i in range(len(combos)):
        send_rows(chunks - 1, i).start()

    for i in range(len(combos)):
        send_filled(i).wait_recv()
    forward_filled().start()

    def collect(ch):
        for i in range(len(combos)):
            send_rows(ch, i).wait_recv()
        forward_rows(ch).start()

    def multiply(ch, first):
        forward_rows(ch).wait_recv()
        for copy in load_weights(ch):
            copy.wait()
        part = pl.ds(pl.multiple_of(ch * CHUNK, CHUNK), CHUNK)
        x = X[ch]
        for W, A in ((WG, AG), (WU, AU)):
            product = jnp.dot(x, W[part, :], preferred_element_type=jnp.float32)
            A[...] = product if first else A[...] + product

    collect(0)
    collect(1)
    multiply(0, True)

    forward_filled().wait()
    total = jnp.sum(OX[...].astype(jnp.float32), axis=0, keepdims=True)
    CNT[z] = jnp.broadcast_to(total, (8, LANES))

    def step(ch, _):
        collect(ch + 1)
        multiply(ch, False)
        return 0

    lax.fori_loop(1, chunks - 1, step, 0)

    def send_count(dz):
        return pltpu.make_async_remote_copy(
            src_ref=CNT.at[z], dst_ref=CNT.at[z],
            send_sem=n_send.at[dz - 1], recv_sem=n_recv.at[dz - 1],
            device_id=(me, (z + dz) % replicas), device_id_type=MESH)

    for dz in range(1, replicas):
        send_count(dz).start()
    multiply(chunks - 1, False)

    def activate(i, top):
        part = pl.ds(pl.multiple_of(i * ROWS, ROWS), ROWS)
        g = AG[part, :]
        h = g / (1.0 + jnp.exp(-g)) * AU[part, :]
        H[part, :] = h
        return jnp.maximum(top, jnp.max(jnp.abs(h).reshape(ROWS // 8, 8, width), axis=0))

    top = lax.fori_loop(0, rows // ROWS, activate, jnp.zeros((8, width), jnp.float32))
    ceiling = jnp.max(top, axis=0, keepdims=True) + EPSILON
    scale = 2.0 / ceiling
    mine = pl.ds(pl.multiple_of(me * width, width), width)

    def send_hidden(i):
        j = other(*alls[i])
        return pltpu.make_async_remote_copy(
            src_ref=H.at[block(j), :], dst_ref=HB.at[:, mine],
            send_sem=h_send.at[i], recv_sem=h_recv.at[i],
            device_id=(j, z), device_id_type=MESH)

    def send_level(i):
        return pltpu.make_async_remote_copy(
            src_ref=LS, dst_ref=LV.at[:, mine],
            send_sem=l_send.at[i], recv_sem=l_recv.at[i],
            device_id=(other(*alls[i]), z), device_id_type=MESH)

    def send_sketch(dz, part):
        return pltpu.make_async_remote_copy(
            src_ref=SK.at[z, part], dst_ref=SK.at[z, part],
            send_sem=s_send.at[dz - 1, part], recv_sem=s_recv.at[dz - 1, part],
            device_id=(me, (z + dz) % replicas), device_id_type=MESH)

    keep_hidden = pltpu.make_async_copy(H.at[block(me), :], HB.at[:, mine], own_sem.at[0])
    keep_level = pltpu.make_async_copy(LS, LV.at[:, mine], own_sem.at[1])
    pair = tiles // 2

    for l in range(tiles):
        lanes = slice(l * LANES, (l + 1) * LANES)
        scale_l = scale[:, lanes]

        def sketch(i, sums):
            part = pl.ds(pl.multiple_of(i * ROWS, ROWS), ROWS)
            scaled = jnp.abs(H[part, lanes]) * scale_l - 1.0
            double = 2.0 * scaled
            previous = OX[part, :].astype(jnp.float32)
            current = previous * scaled
            new = []
            for k in range(KMOM - 1):
                new.append(sums[k] + jnp.sum(current.reshape(ROWS // 8, 8, LANES), axis=0))
                previous, current = current, double * current - previous
            return tuple(new)

        zero = jnp.zeros((8, LANES), jnp.float32)
        sums = lax.fori_loop(0, rows // ROWS, sketch, (zero,) * (KMOM - 1))
        at = l % pair
        SK[z, l // pair, at:at + 1, :] = ceiling[:, lanes]
        for k in range(1, KMOM):
            SK[z, l // pair, k * pair + at:k * pair + at + 1, :] = jnp.sum(
                sums[k - 1], axis=0, keepdims=True)
        if l == pair:
            for dz in range(1, replicas):
                send_sketch(dz, 0).start()
            for i in range(len(alls))[::-1]:
                send_hidden(i).start()
            keep_hidden.start()

    for dz in range(1, replicas):
        send_sketch(dz, 1).start()
    for dz in range(1, replicas):
        send_count(dz).wait()
    for dz in range(1, replicas):
        for part in range(2):
            send_sketch(dz, part).wait()

    def across(k):
        return [
            jnp.concatenate(
                [SK[r, part, k * pair:(k + 1) * pair, :] for part in range(2)], axis=0)
            for r in range(replicas)
        ]

    local = across(0)
    common = functools.reduce(jnp.maximum, local)
    ratio = jnp.concatenate([value / common for value in local], axis=0)
    moments = [jnp.concatenate([CNT[r, :tiles, :] for r in range(replicas)], axis=0)]
    moments += [jnp.concatenate(across(k), axis=0) for k in range(1, KMOM)]

    def added(value):
        return functools.reduce(
            jnp.add, [value[r * tiles:(r + 1) * tiles] for r in range(replicas)])

    weight = 1.0 / added(moments[0])
    level = clip_fraction([added(value) * weight for value in rebase(moments, ratio)])
    level = common * level
    for l in range(tiles):
        LS[0:1, l * LANES:(l + 1) * LANES] = level[l:l + 1]
        LS[1:2, l * LANES:(l + 1) * LANES] = common[l:l + 1]
    for i in range(len(alls)):
        send_hidden(i).wait()
    keep_hidden.wait()
    for i in range(len(alls))[::-1]:
        send_level(i).start()
    keep_level.start()

    def drain(ch, _):
        for i in range(len(combos)):
            send_rows(ch, i).wait_send()
        forward_rows(ch).wait_send()
        return 0

    lax.fori_loop(0, chunks, drain, 0)
    for i in range(len(combos)):
        send_filled(i).wait_send()
    keep_level.wait()
    for i in range(len(alls)):
        send_level(i).wait()


def shards(tokens, routes, gate_weight, up_weight):
    devices = lax.axis_size("expert")
    replicas = lax.axis_size("replica")
    groups = devices // HSPLIT
    count, depth = tokens.shape
    width = gate_weight.shape[1]
    chunks = depth // CHUNK
    rows = devices * CAP
    near = devices // 2 - 1
    tiles = width // LANES
    bf16, f32 = jnp.bfloat16, jnp.float32
    dma = pltpu.SemaphoreType.DMA
    offchip = pl.BlockSpec(memory_space=pltpu.HBM)
    onchip = pl.BlockSpec(memory_space=pltpu.VMEM)
    hidden, levels = pl.pallas_call(
        functools.partial(kernel, devices, replicas, chunks),
        out_shape=(
            jax.ShapeDtypeStruct((CAP, devices * width), f32),
            jax.ShapeDtypeStruct((2, devices * width), f32),
        ),
        in_specs=[offchip] * 4,
        out_specs=(onchip, onchip),
        scratch_shapes=[
            pltpu.VMEM((chunks, count, CHUNK), bf16),
            pltpu.VMEM((routes.shape[1], count), jnp.int32),
            pltpu.VMEM((groups * CAP, count), bf16),
            pltpu.VMEM((chunks, groups * CAP, CHUNK), bf16),
            pltpu.VMEM((groups * CAP, LANES), bf16),
            pltpu.VMEM((chunks, rows, CHUNK), bf16),
            pltpu.VMEM((rows, LANES), bf16),
            pltpu.VMEM((depth, width), bf16),
            pltpu.VMEM((depth, width), bf16),
            pltpu.VMEM((rows, width), f32),
            pltpu.VMEM((rows, width), f32),
            pltpu.VMEM((rows, width), f32),
            pltpu.VMEM((replicas, 2, KMOM * tiles // 2, LANES), f32),
            pltpu.VMEM((replicas, 8, LANES), f32),
            pltpu.VMEM((2, width), f32),
            dma((chunks,)), dma(()), dma((chunks,)), dma((chunks,)),
            dma((chunks, near)), dma((chunks, near)), dma((near,)), dma((near,)),
            dma((chunks,)), dma((chunks,)), dma((2,)),
            dma((replicas - 1, 2)), dma((replicas - 1, 2)),
            dma((replicas - 1,)), dma((replicas - 1,)),
            dma((devices - 1,)), dma((devices - 1,)),
            dma((devices - 1,)), dma((devices - 1,)), dma((2,)),
        ],
        compiler_params=pltpu.CompilerParams(
            collective_id=0, has_side_effects=True, vmem_limit_bytes=62 * 1024 * 1024),
    )(tokens, routes.T, gate_weight, up_weight)
    level, ceiling = levels[0:1], levels[1:2]
    return (jnp.minimum(jnp.maximum(hidden, -level), level) / ceiling).astype(bf16)


def solution(mesh):
    in_specs = (
        P(("expert", "replica"), None),
        P(("expert", "replica"), None),
        P(None, "expert"),
        P(None, "expert"),
    )
    out_specs = P(("expert", "replica"), None)
    return jax.shard_map(shards, mesh=mesh, in_specs=in_specs, out_specs=out_specs, check_vma=False)
```

```python
import functools
import math

import jax
import jax.numpy as jnp
from jax import lax
from jax.experimental import pallas as pl
from jax.experimental.pallas import tpu as pltpu
from jax.sharding import PartitionSpec as P

HSPLIT = 4
CAP = 16
KMOM = 12
QITERS = 4
LANES = 128
CHUNK = 1024
ROWS = 32

QUANTILE_LEVEL = 0.99
EPSILON = 1e-06
MESH = pl.DeviceIdType.MESH

PI_HIGH = 3.140625
PI_LOW = math.pi - PI_HIGH
SIN_TERMS = [(-1.0) ** i / math.factorial(2 * i + 1) for i in range(7)]
COS_TERMS = [(-1.0) ** i / math.factorial(2 * i) for i in range(8)]


def horner(square, terms):
    total = jnp.full_like(square, terms[-1])
    for term in terms[-2::-1]:
        total = total * square + term
    return total


def sin_cos(angle):
    turns = jnp.floor(angle * (1.0 / math.pi) + 0.5)
    rest = (angle - turns * PI_HIGH) - turns * PI_LOW
    sign = 1.0 - 2.0 * (turns - 2.0 * jnp.floor(turns * 0.5))
    square = rest * rest
    return sign * rest * horner(square, SIN_TERMS), sign * horner(square, COS_TERMS)


def clip_fraction(coefficient):
    start = (1.0 - QUANTILE_LEVEL) * math.pi
    total = jnp.zeros_like(coefficient[0])
    for k in range(1, KMOM, 2):
        total = total + coefficient[k - 1] * ((1.0 if k % 4 == 1 else -1.0) / k)
    angle = start - 2.0 * total
    for _ in range(QITERS - 1):
        sine, cosine = sin_cos(angle)
        double = 2.0 * cosine
        before, current = jnp.zeros_like(sine), sine
        total = jnp.zeros_like(sine)
        for k in range(1, KMOM):
            total = total + coefficient[k - 1] * (current * (1.0 / k))
            before, current = current, double * current - before
        angle = start - 2.0 * total
    return 0.5 * (1.0 + sin_cos(angle)[1])


def rebase(moments, ratio):
    shift = ratio - 1.0
    before = moments
    current = [
        0.5 * ratio * (before[j + 1] + before[abs(j - 1)]) + shift * before[j]
        for j in range(KMOM - 1)
    ]
    out = [current[0]]
    twice = 2.0 * shift
    for k in range(1, KMOM - 1):
        following = [
            ratio * (current[j + 1] + current[abs(j - 1)]) + twice * current[j] - before[j]
            for j in range(KMOM - 1 - k)
        ]
        before, current = current, following
        out.append(current[0])
    return out


def kernel(
    devices, replicas, chunks,
    tok, rt, wg, wu, out,
    T, RT, SEL, Y, OY, X, OX, WG, WU, AG, AU, H, SK, CNT, RES,
    tok_sem, rt_sem, wg_sem, wu_sem,
    x_send, x_recv, o_send, o_recv, f_send, f_recv, fo_sem,
    s_send, s_recv, n_send, n_recv, r_send, r_recv, own_sem,
):
    groups = devices // HSPLIT
    half = devices // 2 * CAP
    width = WG.shape[1]
    tiles = width // LANES
    rows = devices * CAP
    me = lax.axis_index("expert")
    z = lax.axis_index("replica")
    c = me % 2
    p = (me // 2) % 2
    a = me // HSPLIT
    partner = me + 1 - 2 * c

    def pos(j):
        return (j % 2) * (devices // 2) + j // 2

    def other(dg, dp, dc):
        return HSPLIT * ((a + dg) % groups) + 2 * ((p + dp) % 2) + (c + dc) % 2

    combos = [(dg, dp) for dg in range(groups) for dp in range(2) if (dg, dp) != (0, 0)]
    combos = combos[::-1]
    alls = [
        (dg, dp, dc)
        for dg in range(groups) for dp in range(2) for dc in range(2)
        if (dg, dp, dc) != (0, 0, 0)
    ]

    def block(j):
        return pl.ds(pl.multiple_of(pos(j) * CAP, CAP), CAP)

    def load_tokens(ch):
        return pltpu.make_async_copy(
            tok.at[:, pl.ds(pl.multiple_of(ch * CHUNK, CHUNK), CHUNK)], T.at[ch], tok_sem.at[ch])

    def load_weights(ch):
        part = pl.ds(pl.multiple_of(ch * CHUNK, CHUNK), CHUNK)
        return (
            pltpu.make_async_copy(wg.at[part], WG.at[part], wg_sem.at[ch]),
            pltpu.make_async_copy(wu.at[part], WU.at[part], wu_sem.at[ch]),
        )

    load_routes = pltpu.make_async_copy(rt, RT, rt_sem)
    load_routes.start()
    for ch in range(chunks):
        load_tokens(ch).start()

    barrier = pltpu.get_barrier_semaphore()
    for combo in alls:
        pl.semaphore_signal(barrier, inc=1, device_id=(other(*combo), z), device_id_type=MESH)
    for dz in range(1, replicas):
        pl.semaphore_signal(
            barrier, inc=1, device_id=(me, (z + dz) % replicas), device_id_type=MESH)

    for ch in range(chunks):
        for copy in load_weights(ch):
            copy.start()

    load_routes.wait()
    routes = RT[...]
    count = routes.shape[1]
    t_from = lax.broadcasted_iota(jnp.int32, (count, count), 0)
    t_to = lax.broadcasted_iota(jnp.int32, (count, count), 1)
    earlier = jnp.where(t_from < t_to, 1.0, 0.0).astype(jnp.bfloat16)
    named = [
        jnp.sum(jnp.where(routes == (a + dg) % groups, 1.0, 0.0), axis=0, keepdims=True)
        for dg in range(groups)
    ]
    table = jnp.concatenate(
        [jnp.broadcast_to(n, (CAP, count)) for n in named], axis=0)
    before = jnp.dot(table.astype(jnp.bfloat16), earlier, preferred_element_type=jnp.float32)
    slot = (lax.broadcasted_iota(jnp.int32, (groups * CAP, count), 0) % CAP).astype(jnp.float32)
    picks = jnp.where(before == slot, table, 0.0)
    SEL[...] = picks.astype(jnp.bfloat16)
    filled = jnp.broadcast_to(
        jnp.sum(picks, axis=1, keepdims=True), (groups * CAP, LANES)).astype(jnp.bfloat16)
    OY[...] = filled
    OX[block(me), :] = filled[:CAP]

    def gather(ch):
        load_tokens(ch).wait()
        picked = jnp.dot(
            SEL[...], T[ch], preferred_element_type=jnp.float32).astype(jnp.bfloat16)
        Y[ch] = picked
        X[ch, block(me), :] = picked[:CAP]

    def send_rows(ch, i):
        dg, dp = combos[i]
        return pltpu.make_async_remote_copy(
            src_ref=Y.at[ch, pl.ds(dg * CAP, CAP), :], dst_ref=X.at[ch, block(me), :],
            send_sem=x_send.at[ch, i], recv_sem=x_recv.at[ch, i],
            device_id=(other(dg, dp, 0), z), device_id_type=MESH)

    def send_filled(i):
        dg, dp = combos[i]
        return pltpu.make_async_remote_copy(
            src_ref=OY.at[pl.ds(dg * CAP, CAP), :], dst_ref=OX.at[block(me), :],
            send_sem=o_send.at[i], recv_sem=o_recv.at[i],
            device_id=(other(dg, dp, 0), z), device_id_type=MESH)

    def forward_rows(ch):
        part = pl.ds(pl.multiple_of(c * half, half), half)
        return pltpu.make_async_remote_copy(
            src_ref=X.at[ch, part, :], dst_ref=X.at[ch, part, :],
            send_sem=f_send.at[ch], recv_sem=f_recv.at[ch],
            device_id=(partner, z), device_id_type=MESH)

    def forward_filled():
        part = pl.ds(pl.multiple_of(c * half, half), half)
        return pltpu.make_async_remote_copy(
            src_ref=OX.at[part, :], dst_ref=OX.at[part, :],
            send_sem=fo_sem.at[0], recv_sem=fo_sem.at[1],
            device_id=(partner, z), device_id_type=MESH)

    gather(0)
    pl.semaphore_wait(barrier, len(alls) + replicas - 1)
    for i in range(len(combos)):
        send_filled(i).start()

    def sending(ch, _):
        gather(ch + 1)
        for i in range(len(combos)):
            send_rows(ch, i).start()
        return 0

    lax.fori_loop(0, chunks - 1, sending, 0)
    for i in range(len(combos)):
        send_rows(chunks - 1, i).start()

    for i in range(len(combos)):
        send_filled(i).wait_recv()
    forward_filled().start()

    def collect(ch):
        for i in range(len(combos)):
            send_rows(ch, i).wait_recv()
        forward_rows(ch).start()

    def multiply(ch, first):
        forward_rows(ch).wait_recv()
        for copy in load_weights(ch):
            copy.wait()
        part = pl.ds(pl.multiple_of(ch * CHUNK, CHUNK), CHUNK)
        x = X[ch]
        for W, A in ((WG, AG), (WU, AU)):
            product = jnp.dot(x, W[part, :], preferred_element_type=jnp.float32)
            A[...] = product if first else A[...] + product

    collect(0)
    collect(1)
    multiply(0, True)

    forward_filled().wait()
    total = jnp.sum(OX[...].astype(jnp.float32), axis=0, keepdims=True)
    CNT[z] = jnp.broadcast_to(total, (8, LANES))

    def step(ch, _):
        collect(ch + 1)
        multiply(ch, False)
        return 0

    lax.fori_loop(1, chunks - 1, step, 0)

    def send_count(dz):
        return pltpu.make_async_remote_copy(
            src_ref=CNT.at[z], dst_ref=CNT.at[z],
            send_sem=n_send.at[dz - 1], recv_sem=n_recv.at[dz - 1],
            device_id=(me, (z + dz) % replicas), device_id_type=MESH)

    for dz in range(1, replicas):
        send_count(dz).start()
    multiply(chunks - 1, False)

    def activate(i, top):
        part = pl.ds(pl.multiple_of(i * ROWS, ROWS), ROWS)
        g = AG[part, :]
        h = g / (1.0 + jnp.exp(-g)) * AU[part, :]
        H[part, :] = h
        return jnp.maximum(top, jnp.max(jnp.abs(h).reshape(ROWS // 8, 8, width), axis=0))

    top = lax.fori_loop(0, rows // ROWS, activate, jnp.zeros((8, width), jnp.float32))
    ceiling = jnp.max(top, axis=0, keepdims=True) + EPSILON
    scale = 2.0 / ceiling
    for l in range(tiles):
        lanes = slice(l * LANES, (l + 1) * LANES)
        scale_l = scale[:, lanes]

        def sketch(i, sums):
            part = pl.ds(pl.multiple_of(i * ROWS, ROWS), ROWS)
            scaled = jnp.abs(H[part, lanes]) * scale_l - 1.0
            double = 2.0 * scaled
            previous = OX[part, :].astype(jnp.float32)
            current = previous * scaled
            new = []
            for k in range(KMOM - 1):
                new.append(sums[k] + jnp.sum(current.reshape(ROWS // 8, 8, LANES), axis=0))
                previous, current = current, double * current - previous
            return tuple(new)

        zero = jnp.zeros((8, LANES), jnp.float32)
        sums = lax.fori_loop(0, rows // ROWS, sketch, (zero,) * (KMOM - 1))
        SK[z, l:l + 1, :] = ceiling[:, lanes]
        for k in range(1, KMOM):
            SK[z, k * tiles + l:k * tiles + l + 1, :] = jnp.sum(
                sums[k - 1], axis=0, keepdims=True)

    def send_sketch(dz):
        return pltpu.make_async_remote_copy(
            src_ref=SK.at[z], dst_ref=SK.at[z],
            send_sem=s_send.at[dz - 1], recv_sem=s_recv.at[dz - 1],
            device_id=(me, (z + dz) % replicas), device_id_type=MESH)

    for dz in range(1, replicas):
        send_sketch(dz).start()
    for dz in range(1, replicas):
        send_count(dz).wait()
    for dz in range(1, replicas):
        send_sketch(dz).wait()

    def across(k):
        return [SK[r, k * tiles:(k + 1) * tiles, :] for r in range(replicas)]

    local = across(0)
    common = functools.reduce(jnp.maximum, local)
    ratio = jnp.concatenate([value / common for value in local], axis=0)
    moments = [jnp.concatenate([CNT[r, :tiles, :] for r in range(replicas)], axis=0)]
    moments += [jnp.concatenate(across(k), axis=0) for k in range(1, KMOM)]

    def added(value):
        return functools.reduce(
            jnp.add, [value[r * tiles:(r + 1) * tiles] for r in range(replicas)])

    weight = 1.0 / added(moments[0])
    level = clip_fraction([added(value) * weight for value in rebase(moments, ratio)])
    level = common * level
    inverse = 1.0 / common

    for l in range(tiles):
        lanes = slice(l * LANES, (l + 1) * LANES)
        bound = level[l:l + 1]
        factor = inverse[l:l + 1]

        def finish(i, _):
            part = pl.ds(pl.multiple_of(i * ROWS, ROWS), ROWS)
            h = jnp.minimum(jnp.maximum(H[part, lanes], -bound), bound)
            RES[part, lanes] = (h * factor).astype(jnp.bfloat16)
            return 0

        lax.fori_loop(0, rows // ROWS, finish, 0)

    mine = pl.ds(pl.multiple_of(me * width, width), width)

    def send_result(i):
        j = other(*alls[i])
        return pltpu.make_async_remote_copy(
            src_ref=RES.at[block(j), :], dst_ref=out.at[:, mine],
            send_sem=r_send.at[i], recv_sem=r_recv.at[i],
            device_id=(j, z), device_id_type=MESH)

    for i in range(len(alls))[::-1]:
        send_result(i).start()
    keep = pltpu.make_async_copy(RES.at[block(me), :], out.at[:, mine], own_sem)
    keep.start()

    def drain(ch, _):
        for i in range(len(combos)):
            send_rows(ch, i).wait_send()
        forward_rows(ch).wait_send()
        return 0

    lax.fori_loop(0, chunks, drain, 0)
    for i in range(len(combos)):
        send_filled(i).wait_send()
    keep.wait()
    for i in range(len(alls)):
        send_result(i).wait()


def shards(tokens, routes, gate_weight, up_weight):
    devices = lax.axis_size("expert")
    replicas = lax.axis_size("replica")
    groups = devices // HSPLIT
    count, depth = tokens.shape
    width = gate_weight.shape[1]
    chunks = depth // CHUNK
    rows = devices * CAP
    near = devices // 2 - 1
    tiles = width // LANES
    bf16, f32 = jnp.bfloat16, jnp.float32
    dma = pltpu.SemaphoreType.DMA
    anywhere = pl.BlockSpec(memory_space=pl.ANY)
    return pl.pallas_call(
        functools.partial(kernel, devices, replicas, chunks),
        out_shape=jax.ShapeDtypeStruct((CAP, devices * width), bf16),
        in_specs=[anywhere] * 4,
        out_specs=pl.BlockSpec(memory_space=pltpu.VMEM),
        scratch_shapes=[
            pltpu.VMEM((chunks, count, CHUNK), bf16),
            pltpu.VMEM((routes.shape[1], count), jnp.int32),
            pltpu.VMEM((groups * CAP, count), bf16),
            pltpu.VMEM((chunks, groups * CAP, CHUNK), bf16),
            pltpu.VMEM((groups * CAP, LANES), bf16),
            pltpu.VMEM((chunks, rows, CHUNK), bf16),
            pltpu.VMEM((rows, LANES), bf16),
            pltpu.VMEM((depth, width), bf16),
            pltpu.VMEM((depth, width), bf16),
            pltpu.VMEM((rows, width), f32),
            pltpu.VMEM((rows, width), f32),
            pltpu.VMEM((rows, width), f32),
            pltpu.VMEM((replicas, KMOM * tiles, LANES), f32),
            pltpu.VMEM((replicas, 8, LANES), f32),
            pltpu.VMEM((rows, width), bf16),
            dma((chunks,)), dma(()), dma((chunks,)), dma((chunks,)),
            dma((chunks, near)), dma((chunks, near)), dma((near,)), dma((near,)),
            dma((chunks,)), dma((chunks,)), dma((2,)),
            dma((replicas - 1,)), dma((replicas - 1,)),
            dma((replicas - 1,)), dma((replicas - 1,)),
            dma((devices - 1,)), dma((devices - 1,)), dma(()),
        ],
        compiler_params=pltpu.CompilerParams(
            collective_id=0, has_side_effects=True, vmem_limit_bytes=53 * 1024 * 1024),
    )(tokens, routes.T, gate_weight, up_weight)


def solution(mesh):
    in_specs = (
        P(("expert", "replica"), None),
        P(("expert", "replica"), None),
        P(None, "expert"),
        P(None, "expert"),
    )
    out_specs = P(("expert", "replica"), None)
    return jax.shard_map(shards, mesh=mesh, in_specs=in_specs, out_specs=out_specs, check_vma=False)
```
